32 devices in a mesh: row: 8 (over y, x, core), col: 4 (over z).
Axes of the slice: x: 2, y: 2, z: 4, core: 2. Of those that a mesh axis runs over, the one named last changes fastest.
Arguments:
- vectors: bfloat16 [32768, 64], P(('row', 'col')), may hold values from -6 to 6
- cotangent: bfloat16 [32768, 64], P(('row', 'col')), may hold values from -360 to 360, as said below
- gap_weights: float32 [64, 64], replicated, as said below
- row_tile: int32 [8, 4, 128], P('row', 'col'), may hold values from -1 to 31, as said below
- col_tile: int32 [8, 4, 128], P('row', 'col'), may hold values from -1 to 63, as said below
Outputs:
- tile_grads: bfloat16 [8, 4, 128, 128, 128], P('row', 'col')
The draws below stay inside these ranges and needn't reach their ends.
Inputs may be any that keep to these rules, and one draw needn't show every extreme that they name: `cotangent`: fresh draw of one law: entries of order one times a row scale rising along the vertices and a column scale per eigenvector. `gap_weights`: Positive, within a factor of 5 of 0.00125 / sqrt(32768). Used slots come first in each cell and name distinct tiles there; row_tile and col_tile are -1 together in padding slots; some cell uses all 128 slots. `col_tile`: padding slots are -1, as in row_tile.
All inputs are finite; a program needn't handle non-finite values.
Results may differ from the reference program's by a relative error of at most 0.011.
Values may be sent and summed in bfloat16 or wider, within the bound.
No kernel may reach another device: no remote copies, remote signals or barrier semaphores. Data moves between devices by JAX's collectives and lax.ppermute only.
A program may use at most 64 MiB of HBM per device.

```python
import math
import jax
import jax.numpy as jnp
from jax import lax

EIGS = 64
TILE = 128
VDEV = 1024
TILES = 128
GRID_ROWS = 8
GRID_COLS = 4
NVERT = 32768
ROWBLK = 32
COLBLK = 64


def draw_cotangent(key, part):
    base_key, jitter_key, column_key = jax.random.split(jax.random.fold_in(key, 11), 3)
    position = jnp.arange(NVERT, dtype=jnp.float32) / NVERT
    jitter = jnp.exp(jax.random.uniform(jitter_key, (NVERT, 1), jnp.float32, 0.0, math.log(2.0)))
    column_scale = jnp.exp(jax.random.uniform(column_key, (1, EIGS), jnp.float32, 0.0, math.log(10.0)))
    base = jnp.clip(jax.random.normal(base_key, (NVERT, EIGS), jnp.float32), -6.0, 6.0)
    row_scale = jnp.power(3.0, position)[:, None] * jitter
    return (base * row_scale * column_scale).astype(jnp.bfloat16)


def draw_gap_weights(key, part):
    center = 0.00125 / math.sqrt(NVERT)
    spread = jax.random.uniform(jax.random.fold_in(key, 21), (EIGS, EIGS), jnp.float32, -math.log(3.0), math.log(3.0))
    return (center * jnp.exp(spread)).astype(jnp.float32)


def tile_lists(key):
    count_key, full_key, pick_key = jax.random.split(jax.random.fold_in(key, 31), 3)
    cells = GRID_ROWS * GRID_COLS
    positions = ROWBLK * COLBLK
    counts = jax.random.randint(count_key, (cells,), max(TILES // 4, 1), TILES + 1)
    full_cell = jax.random.randint(full_key, (), 0, cells)
    counts = jnp.where(jnp.arange(cells) == full_cell, TILES, counts)
    cell_keys = jax.random.split(pick_key, cells)
    picks = jax.vmap(lambda subkey: jax.random.permutation(subkey, positions)[:TILES])(cell_keys)
    used = jnp.arange(TILES)[None, :] < counts[:, None]
    rows_out = jnp.where(used, picks // COLBLK, -1).astype(jnp.int32)
    cols_out = jnp.where(used, picks % COLBLK, -1).astype(jnp.int32)
    return (rows_out.reshape(GRID_ROWS, GRID_COLS, TILES), cols_out.reshape(GRID_ROWS, GRID_COLS, TILES))


def draw_row_tile(key, part):
    return tile_lists(key)[0]


def draw_col_tile(key, part):
    return tile_lists(key)[1]


def block_levels(own_key, dims, shards, low, largest):
    def one(dim, shards_of):
        draws = jax.random.uniform(jax.random.fold_in(jax.random.fold_in(own_key, 6), dim), (shards_of,), jnp.float32, low / len(shards), largest / len(shards))
        return jnp.repeat(jnp.exp(draws), dims[dim] // shards_of).reshape((-1,) + (1,) * (len(dims) - dim - 1))

    level = one(*shards[0])
    for cut in shards[1:]:
        level = level * one(*cut)
    return level


def scatter_about(stream_key, extent, scale, most, pieces=(), kind=jnp.bfloat16):
    drawn = jax.random.normal(stream_key, extent, jnp.float32) * scale
    if len(pieces) > 0:
        drawn = block_levels(stream_key, extent, pieces, -0.22, 0.18) * drawn
    return jnp.clip(drawn, min=-most, max=most).astype(kind)


def setup_inputs(seed: int = 0) -> dict:
    splits = jax.random.split(jax.random.key(seed), 6)
    vectors = scatter_about(splits[0], (NVERT, EIGS), 1.0, 6.0, ((0, 32),))
    cotangent = draw_cotangent(jax.random.fold_in(splits[5], 71), 0)
    gap_weights = draw_gap_weights(jax.random.fold_in(splits[5], 71), 0)
    row_tile = draw_row_tile(jax.random.fold_in(splits[5], 71), 0)
    col_tile = draw_col_tile(jax.random.fold_in(splits[5], 71), 0)
    return dict(vectors=vectors, cotangent=cotangent, gap_weights=gap_weights, row_tile=row_tile, col_tile=col_tile)


def reference(vectors, cotangent, gap_weights, row_tile, col_tile):
    gram = jnp.dot(vectors.T, cotangent, preferred_element_type=jnp.float32)
    scaled = gap_weights * gram
    scaled_hi = scaled.astype(jnp.bfloat16)
    scaled_lo = (scaled - scaled_hi.astype(jnp.float32)).astype(jnp.bfloat16)
    mixed = (jnp.dot(vectors, scaled_hi, preferred_element_type=jnp.float32) + jnp.dot(vectors, scaled_lo, preferred_element_type=jnp.float32)).astype(jnp.bfloat16)
    left_blocks = jnp.concatenate([mixed, vectors], axis=1).reshape(-1, TILE, 2 * EIGS)
    right_blocks = jnp.concatenate([vectors, mixed], axis=1).reshape(-1, TILE, 2 * EIGS)
    per_dev = VDEV // TILE

    def one_cell(device_index):
        grid_row = device_index // GRID_COLS
        grid_col = device_index % GRID_COLS
        rows_here = row_tile[grid_row, grid_col]
        cols_here = col_tile[grid_row, grid_col]
        valid_slot = rows_here >= 0
        row_global = (grid_row * ROWBLK + jnp.maximum(rows_here, 0)).astype(jnp.int32)
        col_local = jnp.maximum(cols_here, 0)
        col_global = (((col_local // per_dev) * GRID_COLS + grid_col) * per_dev + col_local % per_dev).astype(jnp.int32)
        left_part = left_blocks[row_global].astype(jnp.float32)
        right_part = right_blocks[col_global].astype(jnp.float32)
        product = jnp.einsum('gik,gjk->gij', left_part, right_part)
        return jnp.where(valid_slot[:, None, None], product, 0.0).astype(jnp.bfloat16)

    tiles_all = lax.map(one_cell, jnp.arange(GRID_ROWS * GRID_COLS, dtype=jnp.int32))
    return tiles_all.reshape(GRID_ROWS, GRID_COLS, TILES, TILE, TILE)
```

```python
import functools

import jax
import jax.numpy as jnp
from jax import lax
from jax.experimental import pallas as pl
from jax.experimental.pallas import tpu as pltpu
from jax.sharding import PartitionSpec as P

SIDE = 128


def swap(value, axis, step, size):
    return lax.ppermute(value, axis, [(i, i ^ step) for i in range(size)])


def total_over(value, axis, size):
    if size & (size - 1):
        return lax.psum(value, axis)
    step = 1
    while step < size:
        value = value + swap(value, axis, step, size)
        step *= 2
    return value


def tiles_kernel(row_count, col_count, row_idx, col_idx, place, total_ref, *refs):
    row_parts = refs[:row_count]
    col_parts = refs[row_count : row_count + col_count]
    out_ref, left, right, tiles, sems = refs[row_count + col_count :]
    eigs, own = row_parts[0].shape
    per_dev = own // SIDE
    slots = out_ref.shape[0]
    total = total_ref[...]
    high = total.astype(jnp.bfloat16)
    low = (total - high.astype(jnp.float32)).astype(jnp.bfloat16)
    for s in range(col_count):
        part = col_parts[s][...]
        for b in range(per_dev):
            right[s * per_dev + b] = part[:, b * SIDE : (b + 1) * SIDE]
    dims = (((0,), (0,)), ((), ()))
    for s in range(row_count):
        part = row_parts[s][...]
        mixed = lax.dot_general(part, high, dims, preferred_element_type=jnp.float32)
        mixed = mixed + lax.dot_general(part, low, dims, preferred_element_type=jnp.float32)
        left[s * per_dev : (s + 1) * per_dev] = mixed.astype(jnp.bfloat16).reshape(per_dev, SIDE, eigs)
    here_row = place[0]
    here_col = place[1]
    chunks = sems.shape[0]
    step = slots // chunks

    def copy(c):
        return pltpu.make_async_copy(
            tiles.at[pl.ds(c * step, step)], out_ref.at[pl.ds(c * step, step)], sems.at[c]
        )

    def chunk(c, carry):
        for t in range(step):
            g = c * step + t
            i = row_idx[g]
            j = col_idx[g]
            kept = i >= 0
            i = jnp.maximum(i, 0)
            j = jnp.maximum(j, 0)
            li = ((i // per_dev) ^ here_col) * per_dev + i % per_dev
            rj = ((j // per_dev) ^ here_row) * per_dev + j % per_dev
            tile = jnp.dot(left[li], right[rj], preferred_element_type=jnp.float32)
            tiles[g] = jnp.where(kept, tile, 0.0).astype(jnp.bfloat16)
        copy(c).start()
        return carry

    lax.fori_loop(0, chunks, chunk, 0)
    for c in range(chunks):
        copy(c).wait()


def body(row_size, col_size, vectors, cotangent, gap_weights, row_tile, col_tile):
    own, eigs = vectors.shape
    flat = vectors.T
    gram = lax.dot_general(flat, cotangent, (((1,), (0,)), ((), ())), preferred_element_type=jnp.float32)
    scaled = gap_weights * gram
    total = scaled + scaled.T
    row_parts = [flat] + [swap(flat, "col", s, col_size) for s in range(1, col_size)]
    col_parts = [flat] + [swap(flat, "row", s, row_size) for s in range(1, row_size)]
    total = total_over(total, "row", row_size)
    total = total_over(total, "col", col_size)
    slots = row_tile.shape[-1]
    per_dev = own // SIDE
    place = jnp.stack([lax.axis_index("row"), lax.axis_index("col")]).astype(jnp.int32)
    vmem = pl.BlockSpec(memory_space=pltpu.VMEM)
    smem = pl.BlockSpec(memory_space=pltpu.SMEM)
    chunks = 8 if slots % 8 == 0 else 1
    out = pl.pallas_call(
        functools.partial(tiles_kernel, col_size, row_size),
        out_shape=jax.ShapeDtypeStruct((slots, SIDE, SIDE), jnp.bfloat16),
        in_specs=[smem, smem, smem] + [vmem] * (1 + row_size + col_size),
        out_specs=pl.BlockSpec(memory_space=pl.ANY),
        scratch_shapes=[
            pltpu.VMEM((col_size * per_dev, SIDE, eigs), jnp.bfloat16),
            pltpu.VMEM((row_size * per_dev, eigs, SIDE), jnp.bfloat16),
            pltpu.VMEM((slots, SIDE, SIDE), jnp.bfloat16),
            pltpu.SemaphoreType.DMA((chunks,)),
        ],
    )(row_tile.reshape(slots), col_tile.reshape(slots), place, total, *row_parts, *col_parts)
    return out.reshape(1, 1, slots, SIDE, SIDE)


def solution(mesh):
    return jax.shard_map(
        functools.partial(body, mesh.shape["row"], mesh.shape["col"]),
        mesh=mesh,
        in_specs=(
            P(("row", "col"), None),
            P(("row", "col"), None),
            P(),
            P("row", "col", None),
            P("row", "col", None),
        ),
        out_specs=P("row", "col", None, None, None),
        check_vma=False,
    )
```
